32 devices in a mesh: dp: 8 (over z, y), tensor: 4 (over x, core).
Axes of the slice: x: 2, y: 2, z: 4, core: 2. Of those that a mesh axis runs over, the one named last changes fastest.
Arguments:
- tokens: bfloat16 [8192, 768], P('dp'), may hold values from -6 to 6
- cotangent: bfloat16 [8192, 768], P('dp'), may hold values from -6 to 6
- gain_attn: float32 [768], replicated, may hold values from 0.5 to 1.5
- prefix_len: int32 [8], P('dp'), may hold values from 102 to 512
- bucket_ids: int32 [2047], replicated, may hold values from 0 to 31
- pos_bias: float32 [32, 12], P(None, 'tensor'), may hold values from -4 to 4
- w_qkv: bfloat16 [3, 768, 768], P(None, None, 'tensor'), may hold values from -0.21875 to 0.21875
- w_attn_out: bfloat16 [768, 768], P('tensor'), may hold values from -2.5 to 2.5
- gain_ffn: float32 [768], replicated, may hold values from 0.5 to 1.5
- w_router: bfloat16 [768, 4], replicated, may hold values from -0.4375 to 0.4375
- expert_ids: int32 [8192, 2], P('dp'), may hold values from 0 to 3, all different within a row; in each aligned block of 1024 rows (0 to 1023, 1024 to 2047, ...) at most 640 rows name the same one
- w_expert_in: bfloat16 [4, 768, 3072], P(None, None, 'tensor'), may hold values from -0.21875 to 0.21875
- w_expert_out: bfloat16 [4, 3072, 768], P(None, 'tensor'), may hold values from -0.21875 to 0.21875
Outputs:
- out: bfloat16 [8192, 768], P('dp', 'tensor')
- grad_tokens: float32 [8192, 768], P('dp', 'tensor')
- grad_gain_attn: float32 [768], P('dp')
- grad_pos_bias: float32 [32, 12], P(None, 'tensor')
- grad_w_qkv: float32 [3, 768, 768], P(None, 'dp', 'tensor')
- grad_w_attn_out: float32 [768, 768], P('tensor', 'dp')
- grad_gain_ffn: float32 [768], P('dp')
- grad_w_router: float32 [768, 4], P('dp')
- grad_w_expert_in: float32 [4, 768, 3072], P(None, 'dp', 'tensor')
- grad_w_expert_out: float32 [4, 3072, 768], P(None, 'tensor', 'dp')
The draws below stay inside these ranges and needn't reach their ends.
Inputs may be any that keep to these rules, and one draw needn't show every extreme that they name: `expert_ids`: each row names two different experts; in the rows of one sequence no expert is named by more than 640 rows.
All inputs are finite; a program needn't handle non-finite values.
Results may differ from the reference program's by a relative error of at most 0.014.
Values sent between devices are 32-bit elements; how exact they have to be, the bound alone decides.
No kernel may reach another device: no remote copies, remote signals or barrier semaphores. Data moves between devices by JAX's collectives and lax.ppermute only.
A program may use at most 192 MiB of HBM per device.

```python
import math
import jax
import jax.numpy as jnp
import numpy as np
from jax import lax

D = 768
HEADS = 12
HD = 64
FF = 3072
EXPERTS = 4
NB = 32
LEN = 1024
CAP = 640
SEQS = 8
TOKENS = 8192


def set_ends(drawn, rng, smallest, top_value):
    longest = drawn.shape.index(max(drawn.shape))
    spots = []
    for shift in (0, 1):
        where = [jax.random.randint(jax.random.fold_in(rng, axis), (), 0, length) for axis, length in enumerate(drawn.shape)]
        where[longest] = (where[longest] + shift) % drawn.shape[longest]
        spots.append(tuple(where))
    return drawn.at[spots[0]].set(smallest).at[spots[1]].set(top_value)


def block_levels(rng, extent, shards, smallest, largest):
    gain = 1.0
    for dim, parts in shards:
        draws = jax.random.uniform(jax.random.fold_in(jax.random.fold_in(rng, 6), dim), (parts,), jnp.float32, smallest / len(shards), largest / len(shards))
        gain = gain * jnp.repeat(jnp.exp(draws), extent[dim] // parts).reshape((-1,) + (1,) * (len(extent) - 1 - dim))
    return gain


def assign_block(own_key, own, number, rows, count, top, reach, skew):
    order = jax.random.permutation(own_key, count)
    crowded, ordinary = portions_of(count, rows * top, reach, skew, True), portions_of(count, rows * top, reach, skew, False)
    places = jnp.arange(count)

    def named(sizes, offset_by):
        used = int((sizes > 0).sum())
        fixed = max(1, used // 4)
        passed = fixed + (places - fixed + offset_by * (used - fixed)) % max(1, count - fixed)
        return jnp.zeros((count,), jnp.int32).at[order[jnp.where(places < fixed, places, passed)]].set(jnp.asarray(sizes, jnp.int32))

    sizes = jnp.where(number % 4 == 0, named(crowded, number // 4), named(ordinary, number - number // 4 - 1))
    mixed = jax.random.permutation(jax.random.fold_in(own, 3), count)
    donor, sink = mixed[0:count // 2 * 2:2], mixed[1:count // 2 * 2:2]
    slack = jnp.minimum(sizes[donor] - 1, reach - sizes[sink]) // 2
    slack = jnp.where((donor == order[0]) | (sink == order[0]) | (sizes[sink] == 0), 0, jnp.maximum(slack, 0))
    passed = jax.random.randint(jax.random.fold_in(own, 4), (count // 2,), 0, 1 << 20) % (slack + 1)
    sizes = sizes.at[donor].add(-passed).at[sink].add(passed)
    labels = jnp.searchsorted(jnp.cumsum(sizes), jnp.arange(rows * top), side="right").astype(jnp.int32)
    listing = labels.reshape(top, rows).T
    listing = listing[jax.random.permutation(jax.random.fold_in(own, 1), rows)]
    offset_by = jax.random.randint(jax.random.fold_in(own, 2), (rows, 1), 0, top)
    return jnp.take_along_axis(listing, (jnp.arange(top)[None, :] + offset_by) % top, axis=1)


def portions_of(amount, total, bound, lean, full):
    loads = [(1 << 20) // math.isqrt(standing ** lean) + 1 for standing in range(1, amount + 1)]
    largest = bound if full else min(bound, max(-(-total // amount), total * loads[0] // sum(loads)))
    least = 1 if total - largest >= amount - 1 else 0
    holding, rest = [largest] + [least] * (amount - 1), total - largest - least * (amount - 1)
    while rest > 0:
        movable = [i for i in range(1, amount) if holding[i] < largest] or [i for i in range(1, amount) if holding[i] < bound]
        pool, left = sum([loads[i] for i in movable]), rest
        for i in movable:
            extra = min(bound - holding[i], max(1, left * loads[i] // pool), rest)
            holding[i] = holding[i] + extra
            rest = rest - extra
    return np.array(holding)


def centred(own_key, dims, width, most, cuts=(), kind=jnp.bfloat16):
    level = block_levels(own_key, dims, cuts, -0.22, 0.18) if cuts else 1.0
    array = jax.random.normal(own_key, dims, jnp.float32) * width * level
    return jnp.minimum(jnp.maximum(array, -most), most).astype(kind)


def setup_inputs(seed: int = 0) -> dict:
    splits = jax.random.split(jax.random.key(seed), 14)
    tokens = centred(splits[0], (TOKENS, D), 1.0, 6.0, ((0, 8),))
    cotangent = centred(splits[1], (TOKENS, D), 1.0, 6.0, ((0, 8),))
    gain_attn = jnp.clip(1.0 + 0.1 * jax.random.normal(splits[2], (D,), jnp.float32), 0.5, 1.5)
    prefix_len = set_ends(jax.random.randint(splits[3], (SEQS,), LEN // 10, LEN // 2 + 1), jax.random.fold_in(splits[3], 1), LEN // 10, (LEN // 2 + 1) - 1).astype(jnp.int32)
    bucket_ids = set_ends(jax.random.randint(splits[4], (2 * LEN - 1,), 0, NB), jax.random.fold_in(splits[4], 1), 0, NB - 1).astype(jnp.int32)
    pos_bias = centred(splits[5], (NB, HEADS), 1.0, 4.0, ((1, 4),), jnp.float32)
    w_qkv = centred(splits[6], (3, D, HEADS * HD), D ** -0.5, 0.21875, ((2, 4),))
    w_attn_out = centred(splits[7], (HEADS * HD, D), (max(1, HEADS * HD // 128)) ** -0.5, 2.5, ((0, 4),))
    gain_ffn = jnp.clip(1.0 + 0.1 * jax.random.normal(splits[8], (D,), jnp.float32), 0.5, 1.5)
    w_router = centred(splits[9], (D, EXPERTS), (D // 4) ** -0.5, 0.4375)
    expert_ids_keys = jax.random.split(jax.random.fold_in(splits[10], 1), TOKENS // LEN)
    expert_ids_turns = jax.random.permutation(jax.random.fold_in(splits[10], 3), TOKENS // LEN)
    expert_ids = jax.vmap(lambda own, number: assign_block(jax.random.fold_in(splits[10], 2), own, number, LEN, EXPERTS, 2, CAP, 1))(expert_ids_keys, expert_ids_turns).reshape((TOKENS, 2))
    w_expert_in = centred(splits[11], (EXPERTS, D, FF), D ** -0.5, 0.21875, ((2, 4),))
    w_expert_out = centred(splits[12], (EXPERTS, FF, D), (FF // 4) ** -0.5, 0.21875, ((1, 4),))
    return dict(tokens=tokens, cotangent=cotangent, gain_attn=gain_attn, prefix_len=prefix_len, bucket_ids=bucket_ids, pos_bias=pos_bias, w_qkv=w_qkv, w_attn_out=w_attn_out, gain_ffn=gain_ffn, w_router=w_router, expert_ids=expert_ids, w_expert_in=w_expert_in, w_expert_out=w_expert_out)


EPS = 1e-06
HIGH = lax.Precision.HIGHEST

@jax.custom_vjp
def low(v):
    return lax.optimization_barrier(v.astype(jnp.bfloat16)).astype(jnp.float32)

@jax.custom_vjp
def low_back(v):
    return v

def low_keep(v):
    return (low(v), None)

def low_pass(kept, grad):
    return (grad,)

def back_keep(v):
    return (v, None)

def back_low(kept, grad):
    return (low(grad),)
low.defvjp(low_keep, low_pass)
low_back.defvjp(back_keep, back_low)

def slot_positions(routes, experts, capacity):
    flat_ids = routes.reshape(-1).astype(jnp.int32)
    marks = (flat_ids[:, None] == jnp.arange(experts, dtype=jnp.int32)[None, :]).astype(jnp.int32)
    before = jnp.cumsum(marks, axis=0, dtype=jnp.int32) - marks
    within = lax.optimization_barrier(jnp.sum(before * marks, axis=1, dtype=jnp.int32))
    return (flat_ids * capacity + within).astype(jnp.int32)

def attend(row_start, block_rows, queries, key_heads, value_heads, bias_table, prefix):
    length = key_heads.shape[1]
    row_ids = row_start + jnp.arange(block_rows, dtype=jnp.int32)
    col_ids = jnp.arange(length, dtype=jnp.int32)
    offsets = (row_ids[:, None] - col_ids[None, :] + (length - 1)).astype(jnp.int32)
    query_rows = lax.dynamic_slice_in_dim(queries, row_start, block_rows, 1)
    scores = jnp.einsum('hqd,hkd->hqk', query_rows, key_heads, precision=HIGH) * 0.125 + bias_table[:, offsets]
    scores = low_back(scores)
    visible = (col_ids[None, :] <= row_ids[:, None]) | (col_ids[None, :] < prefix)
    scores = jnp.where(visible[None], scores, -1e+30)
    softmax_p = jax.nn.softmax(scores, axis=-1)
    return jnp.einsum('hqk,hkd->hqd', low(softmax_p), value_heads, precision=HIGH)

def forward(params, tokens_f, prefix, bucket_ids, routes):
    gain_attn, pos_bias, w_qkv, w_attn_out, gain_ffn, w_router, w_expert_in, w_expert_out = params
    length, model_width = tokens_f.shape
    head_count = pos_bias.shape[1]
    head_size = w_attn_out.shape[0] // head_count
    experts = w_router.shape[1]
    factor1 = lax.rsqrt(lax.optimization_barrier(jnp.mean(tokens_f * tokens_f, axis=1, keepdims=True)) + EPS)
    normed1 = low(tokens_f * factor1 * gain_attn)
    qkv_all = low_back(low(jnp.einsum('ld,cdf->clf', normed1, w_qkv, precision=HIGH)))
    qkv_all = qkv_all.reshape(3, length, head_count, head_size).transpose(0, 2, 1, 3)
    bias_table = pos_bias[bucket_ids].T
    block_rows = min(512, length)
    starts = jnp.arange(length // block_rows, dtype=jnp.int32) * block_rows

    def one_block(row_start):
        return attend(row_start, block_rows, qkv_all[0], qkv_all[1], qkv_all[2], bias_table, prefix)
    blocks = lax.map(jax.checkpoint(one_block), starts)
    attended = blocks.transpose(1, 0, 2, 3).reshape(head_count, length, head_size)
    attended = low_back(low(attended)).transpose(1, 0, 2).reshape(length, head_count * head_size)
    attn_branch = low_back(jnp.dot(attended, w_attn_out, precision=HIGH))
    hidden = tokens_f + attn_branch
    factor2 = lax.rsqrt(lax.optimization_barrier(jnp.mean(hidden * hidden, axis=1, keepdims=True)) + EPS)
    normed2 = low(hidden * factor2 * gain_ffn)
    logits = jnp.dot(normed2, w_router, precision=HIGH)
    softmax_r = jax.nn.softmax(logits, axis=-1)
    chosen = (routes[:, :, None] == jnp.arange(experts, dtype=jnp.int32)[None, None, :]).astype(jnp.float32)
    gate_vals = lax.optimization_barrier(jnp.sum(softmax_r[:, None, :] * chosen, axis=-1))
    capacity = CAP
    slot_index = slot_positions(routes, experts, capacity)
    token_index = jnp.repeat(jnp.arange(length, dtype=jnp.int32), 2)
    dispatched = jnp.zeros((experts * capacity, model_width), jnp.float32).at[slot_index].set(normed2[token_index])
    pre_act = jnp.einsum('ecd,edf->ecf', dispatched.reshape(experts, capacity, model_width), w_expert_in, precision=HIGH)
    activated = low(jax.nn.gelu(low_back(pre_act)))
    expert_rows = low_back(jnp.einsum('ecf,efd->ecd', activated, w_expert_out, precision=HIGH))
    expert_rows = expert_rows.reshape(experts * capacity, model_width)
    picked = expert_rows[slot_index].reshape(length, 2, model_width)
    return hidden + lax.optimization_barrier(jnp.sum(gate_vals[:, :, None] * picked, axis=1))

def reference(tokens, cotangent, gain_attn, prefix_len, bucket_ids, pos_bias, w_qkv, w_attn_out, gain_ffn, w_router, expert_ids, w_expert_in, w_expert_out):
    params = (gain_attn.astype(jnp.float32), pos_bias.astype(jnp.float32), w_qkv.astype(jnp.float32), w_attn_out.astype(jnp.float32), gain_ffn.astype(jnp.float32), w_router.astype(jnp.float32), w_expert_in.astype(jnp.float32), w_expert_out.astype(jnp.float32))
    sequences = tokens.astype(jnp.float32).reshape(SEQS, LEN, D)
    seq_cots = cotangent.astype(jnp.float32).reshape(SEQS, LEN, D)
    seq_routes = expert_ids.reshape(SEQS, LEN, 2)

    def one_sequence(carried, item):
        seq_tokens, seq_cot, prefix, routes = item

        def layer(weights, inputs):
            return forward(weights, inputs, prefix, bucket_ids, routes)
        result, pull = jax.vjp(layer, params, seq_tokens)
        grads, d_tokens = pull(seq_cot)
        carried = jax.tree.map(jnp.add, carried, grads)
        return (carried, (result.astype(jnp.bfloat16), d_tokens))
    zeros = jax.tree.map(jnp.zeros_like, params)
    grads, (outputs, d_all) = lax.scan(one_sequence, zeros, (sequences, seq_cots, prefix_len, seq_routes))
    return (outputs.reshape(TOKENS, D), d_all.reshape(TOKENS, D), grads[0], grads[1], grads[2], grads[3], grads[4], grads[5], grads[6], grads[7])
```

```python
import jax
import jax.numpy as jnp
from jax import lax
from jax.experimental import pallas as pl
from jax.experimental.pallas import tpu as pltpu
from jax.sharding import PartitionSpec as P

EPS = 1e-06
f32, bf16 = jnp.float32, jnp.bfloat16
NN = (((1,), (0,)), ((), ()))
NT = (((1,), (1,)), ((), ()))
TN = (((0,), (0,)), ((), ()))
VM = pl.BlockSpec(memory_space=pltpu.VMEM)
SM = pl.BlockSpec(memory_space=pltpu.SMEM)

CORE = [(0, 1), (1, 0), (2, 3), (3, 2)]
ACROSS = [(0, 2), (2, 0), (1, 3), (3, 1)]


def dot(a, b, dims=NN):
    return lax.dot_general(a, b, dims, preferred_element_type=f32)


def params(mib):
    return pltpu.CompilerParams(vmem_limit_bytes=mib << 20)


def cost(flops, moved):
    return pl.CostEstimate(flops=flops, transcendentals=0, bytes_accessed=moved)


def bucket_hits(ids_ref, buckets):
    ids = ids_ref[...]
    return ids == lax.broadcasted_iota(jnp.int32, (buckets, ids.shape[1]), 0)


def build_band(ids_ref, pb_ref, band):
    width = ids_ref.shape[1]
    hit = bucket_hits(ids_ref, pb_ref.shape[0])
    for h in range(band.shape[0]):
        rev = jnp.sum(jnp.where(hit, pb_ref[:, h : h + 1], 0.0), axis=0, keepdims=True)
        full = jnp.broadcast_to(rev, (128, width))
        band[h, :, :] = pltpu.roll(full, width - 127, 1, stride=1, stride_axis=0)[:, : width - 128]


def attn_fwd_kernel(
    prefix_ref, x_ref, gain_ref, w_ref, ids_ref, pb_ref,
    a_ref, q_ref, kt_ref, v_ref, os_ref, o_ref, band,
):
    heads, length, size = q_ref.shape
    flat = heads * size
    rows_at_once = 256
    build_band(ids_ref, pb_ref, band)

    def project(i, carry):
        rows = pl.ds(pl.multiple_of(i * rows_at_once, rows_at_once), rows_at_once)
        x = x_ref[rows, :].astype(f32)
        r = lax.rsqrt(jnp.mean(x * x, axis=1, keepdims=True) + EPS)
        a = (x * r * gain_ref[...]).astype(bf16)
        a_ref[rows, :] = a
        q = dot(a, w_ref[0]).astype(bf16) * 0.125
        k = dot(a, w_ref[1]).astype(bf16)
        v = dot(a, w_ref[2]).astype(bf16)
        for h in range(heads):
            part = slice(h * size, (h + 1) * size)
            q_ref[h, rows, :] = q[:, part]
            v_ref[h, rows, :] = v[:, part]
            kt_ref[h, :, rows] = k[:, part].T
        return carry

    lax.fori_loop(0, length // rows_at_once, project, 0)
    prefix = prefix_ref[0]
    half = length // 2

    def head(h, carry):
        for b in range(length // rows_at_once):
            nk = max(half, rows_at_once * (b + 1))
            s = dot(q_ref[h, b * rows_at_once : (b + 1) * rows_at_once, :], kt_ref[h, :, 0:nk])
            for sub in range(rows_at_once // 128):
                row0 = b * rows_at_once + sub * 128
                off = length - 128 - row0
                t = s[sub * 128 : (sub + 1) * 128, :] + band[h, :, off : off + nk]
                row = row0 + lax.broadcasted_iota(jnp.int32, (128, 1), 0)
                col = lax.broadcasted_iota(jnp.int32, (128, nk), 1)
                t = jnp.where(col < jnp.maximum(row + 1, prefix), t, -1e30)
                m = jnp.max(t, axis=1, keepdims=True)
                e = jnp.exp(t - m)
                total = jnp.sum(e, axis=1, keepdims=True)
                p = (e * (1.0 / total)).astype(bf16)
                os_ref[h, row0 : row0 + 128, 0:size] = dot(p, v_ref[h, 0:nk, :])
                os_ref[h, row0 : row0 + 128, size : 2 * size] = jnp.broadcast_to(
                    m + jnp.log(total), (128, size)
                )
        return carry

    lax.fori_loop(0, heads, head, 0)
    for h in range(heads):
        o = os_ref[h, :, 0:size].astype(bf16).astype(f32)
        o_ref[:, h * size : (h + 1) * size] = o[:half]
        o_ref[:, flat + h * size : flat + (h + 1) * size] = o[half:]


def attn_fwd(prefix, tokens, gain, w, ids, pb):
    length, width = tokens.shape
    heads = pb.shape[1]
    flat = w.shape[2]
    size = flat // heads
    sds = jax.ShapeDtypeStruct
    return pl.pallas_call(
        attn_fwd_kernel,
        out_shape=(
            sds((length, width), bf16),
            sds((heads, length, size), bf16),
            sds((heads, size, length), bf16),
            sds((heads, length, size), bf16),
            sds((heads, length, 2 * size), f32),
            sds((length // 2, 2 * flat), f32),
        ),
        in_specs=[SM] + [VM] * 5,
        out_specs=[VM] * 6,
        scratch_shapes=[pltpu.VMEM((heads, 128, 2 * length - 128), f32)],
        compiler_params=params(36),
        cost_estimate=cost(12_000_000_000, 8_000_000),
        name="attn_fwd",
    )(prefix, tokens, gain.reshape(1, width), w, ids, pb)


def attn_bwd_kernel(
    prefix_ref, t_ref, d0_ref, d1_ref, d2_ref, d3_ref, wo_ref, q_ref, kt_ref, v_ref, os_ref,
    ids_ref, pb_ref,
    g_ref, dpb_ref, band, dband, do_s, dot_s, qt_s, vt_s, dk_s, dv_s,
):
    heads, length, size = q_ref.shape
    rows_at_once = 256
    width = 2 * length
    half = length // 2
    build_band(ids_ref, pb_ref, band)
    dband[...] = jnp.zeros_like(dband)
    dk_s[...] = jnp.zeros_like(dk_s)
    dv_s[...] = jnp.zeros_like(dv_s)
    count = d0_ref.shape[0]
    for r, d_ref in enumerate((d0_ref, d1_ref, d2_ref, d3_ref)):
        rows = pl.ds(pl.multiple_of((t_ref[0] ^ r) * count, count), count)
        d = d_ref[...].astype(bf16)
        do = dot(d, wo_ref[...], NT).astype(bf16)
        dt = dot(wo_ref[...], d, NT).astype(bf16)
        for h in range(heads):
            do_s[h, rows, :] = do[:, h * size : (h + 1) * size]
            dot_s[h, :, rows] = dt[h * size : (h + 1) * size, :]

    def turn(i, carry):
        rows = pl.ds(pl.multiple_of(i * rows_at_once, rows_at_once), rows_at_once)
        for h in range(heads):
            qt_s[h, :, rows] = q_ref[h, rows, :].T
            vt_s[h, :, rows] = v_ref[h, rows, :].T
        return carry

    lax.fori_loop(0, length // rows_at_once, turn, 0)
    prefix = prefix_ref[0]

    def head(h, carry):
        for b in range(length // rows_at_once):
            nk = max(half, rows_at_once * (b + 1))
            blk = slice(b * rows_at_once, (b + 1) * rows_at_once)
            s = dot(q_ref[h, blk, :], kt_ref[h, :, 0:nk])
            dp = dot(do_s[h, blk, :], vt_s[h, :, 0:nk])
            ps, dss = [], []
            for sub in range(rows_at_once // 128):
                row0 = b * rows_at_once + sub * 128
                off = length - 128 - row0
                part = slice(sub * 128, (sub + 1) * 128)
                t = s[part, :] + band[h, :, off : off + nk]
                row = row0 + lax.broadcasted_iota(jnp.int32, (128, 1), 0)
                col = lax.broadcasted_iota(jnp.int32, (128, nk), 1)
                kept = os_ref[h, row0 : row0 + 128, :]
                t = jnp.where(col < jnp.maximum(row + 1, prefix), t, -1e30)
                p = jnp.exp(t - kept[:, size : size + 1])
                delta = jnp.sum(
                    do_s[h, row0 : row0 + 128, :].astype(f32) * kept[:, :size],
                    axis=1, keepdims=True,
                )
                ds = (p * (dp[part, :] - delta)).astype(bf16)
                dband[h, :, off : off + nk] += ds.astype(f32)
                ps.append(p.astype(bf16))
                dss.append(ds)
            p = jnp.concatenate(ps, 0)
            ds = jnp.concatenate(dss, 0)
            dk_s[h, :, 0:nk] += dot(qt_s[h, :, blk], ds)
            dv_s[h, :, 0:nk] += dot(dot_s[h, :, blk], p)
            g_ref[0, h, :, blk] = (dot(kt_ref[h, :, 0:nk], ds, NT) * 0.125).astype(bf16)
        g_ref[1, h] = dk_s[h].astype(bf16)
        g_ref[2, h] = dv_s[h].astype(bf16)
        return carry

    lax.fori_loop(0, heads, head, 0)
    hit = bucket_hits(ids_ref, dpb_ref.shape[0])
    cols = []
    for h in range(heads):
        d = jnp.concatenate([dband[h], jnp.zeros((128, 128), f32)], axis=1)
        n = 64
        while n >= 8:
            d = pltpu.roll(d[:n], n, 1) + d[n : 2 * n]
            n //= 2
        total = d[7:8]
        for r in range(7):
            total = total + pltpu.roll(d[r : r + 1], 7 - r, 1)
        cols.append(jnp.sum(jnp.where(hit, total, 0.0), axis=1, keepdims=True))
    dpb_ref[...] = jnp.concatenate(cols, axis=1)


def attn_bwd(prefix, t, shards, wo, q, kt, v, os, ids, pb):
    heads, length, size = q.shape
    sds = jax.ShapeDtypeStruct
    return pl.pallas_call(
        attn_bwd_kernel,
        out_shape=(sds((3, heads, size, length), bf16), sds(pb.shape, f32)),
        in_specs=[SM, SM] + [VM] * 11,
        out_specs=[VM] * 2,
        scratch_shapes=[pltpu.VMEM((heads, 128, 2 * length - 128), f32)] * 2
        + [pltpu.VMEM((heads, length, size), bf16)]
        + [pltpu.VMEM((heads, size, length), bf16)] * 3
        + [pltpu.VMEM((heads, size, length), f32)] * 2,
        compiler_params=params(40),
        cost_estimate=cost(12_000_000_000, 8_000_000),
        name="attn_bwd",
    )(prefix, t, *shards, wo, q, kt, v, os, ids, pb)


def proj_kernel(
    x_ref, o0, o1, o2, o3, w0, w1, w2, w3, gain_ref, router_ref, ids_ref,
    h_ref, b_ref, gates_ref, probs_ref,
):
    length = x_ref.shape[0]
    flat = w0.shape[0]
    experts = router_ref.shape[1]
    half = length // 2
    step = 256
    for i in range(length // step):
        rows = slice(i * step, (i + 1) * step)
        top = (i * step) % half
        lane = flat * ((i * step) // half)
        acc = x_ref[rows, :].astype(f32)
        for o, w in ((o0, w0), (o1, w1), (o2, w2), (o3, w3)):
            acc = acc + dot(o[top : top + step, lane : lane + flat].astype(bf16), w[...].astype(bf16))
        h_ref[rows, :] = acc
        r = lax.rsqrt(jnp.mean(acc * acc, axis=1, keepdims=True) + EPS)
        b = (acc * r * gain_ref[...]).astype(bf16)
        b_ref[rows, :] = b
        logits = dot(b, router_ref[...])
        e = jnp.exp(logits - jnp.max(logits, axis=1, keepdims=True))
        probs = e / jnp.sum(e, axis=1, keepdims=True)
        ids = ids_ref[rows, :]
        lanes = lax.broadcasted_iota(jnp.int32, (step, experts), 1)
        chosen = (ids[:, 0:1] == lanes) | (ids[:, 1:2] == lanes)
        gates_ref[rows, :] = jnp.where(chosen, probs, 0.0)
        probs_ref[rows, :] = probs


def proj(tokens, os, ws, gain, router, ids):
    length, width = tokens.shape
    experts = router.shape[1]
    sds = jax.ShapeDtypeStruct
    return pl.pallas_call(
        proj_kernel,
        out_shape=(
            sds((length, width), f32),
            sds((length, width), bf16),
            sds((length, experts), f32),
            sds((length, experts), f32),
        ),
        in_specs=[VM] * 12,
        out_specs=[VM] * 4,
        compiler_params=params(32),
        cost_estimate=cost(1_200_000_000, 14_000_000),
        name="proj",
    )(tokens, *os, *ws, gain.reshape(1, width), router, ids)


def expert_kernel(b_ref, w_ref, c_ref, gates_ref, gg_ref, du_ref, dg_ref, acc, cols):
    i = pl.program_id(0)
    per = pl.num_programs(0) // gates_ref.shape[1]
    e = i // per
    j = i % per
    length = b_ref.shape[0]
    step = 256
    k0 = 0.7978845608028654
    k1 = 0.044715

    def chunk(n, carry):
        rows = pl.ds(pl.multiple_of(n * step, step), step)
        u = dot(b_ref[rows, :], w_ref[...])
        lanes = lax.broadcasted_iota(jnp.int32, (step, gates_ref.shape[1]), 1)
        gate = jnp.sum(jnp.where(lanes == e, gates_ref[rows, :], 0.0), axis=1, keepdims=True)
        u2 = u * u
        t = jnp.tanh(u * (k0 + (k0 * k1) * u2))
        half = 0.5 + 0.5 * t
        g = u * half
        slope = half + (0.5 * u) * (1.0 - t * t) * (k0 + (3.0 * k0 * k1) * u2)
        c = c_ref[rows, :].astype(f32)
        gg_ref[rows, :] = (g * gate).astype(bf16)
        du_ref[rows, :] = (gate * c * slope).astype(bf16)
        cg = c * g
        part = cg[:, 0:128]
        for q in range(1, cg.shape[1] // 128):
            part = part + cg[:, q * 128 : (q + 1) * 128]
        total = jnp.where(j == 0, part, acc[rows, :] + part)
        acc[rows, :] = total

        @pl.when(j == per - 1)
        def _():
            lane = lax.broadcasted_iota(jnp.int32, (step, 128), 1)
            cols[rows, :] = jnp.where(
                lane == e, jnp.sum(total, axis=1, keepdims=True), cols[rows, :]
            )

        return carry

    lax.fori_loop(0, length // step, chunk, 0)

    @pl.when(i == pl.num_programs(0) - 1)
    def _():
        def turn(n, carry):
            rows = pl.ds(pl.multiple_of(n * step, step), step)
            dg_ref[:, rows] = cols[rows, :].T[:8]
            return carry

        lax.fori_loop(0, length // step, turn, 0)


def expert_pass(b, w_in, c, gates):
    length, width = b.shape
    experts, _, hidden = w_in.shape
    block = 256
    per = hidden // block
    sds = jax.ShapeDtypeStruct
    return pl.pallas_call(
        expert_kernel,
        out_shape=(
            sds((length, experts * hidden), bf16),
            sds((length, experts * hidden), bf16),
            sds((8, length), f32),
        ),
        grid_spec=pltpu.PrefetchScalarGridSpec(
            num_scalar_prefetch=0,
            grid=(experts * per,),
            in_specs=[
                pl.BlockSpec((length, width), lambda i: (0, 0)),
                pl.BlockSpec((None, width, block), lambda i: (i // per, 0, i % per)),
                pl.BlockSpec((length, block), lambda i: (0, i)),
                pl.BlockSpec((length, experts), lambda i: (0, 0)),
            ],
            out_specs=[
                pl.BlockSpec((length, block), lambda i: (0, i)),
                pl.BlockSpec((length, block), lambda i: (0, i)),
                pl.BlockSpec((8, length), lambda i: (0, 0)),
            ],
            scratch_shapes=[pltpu.VMEM((length, 128), f32), pltpu.VMEM((length, 128), f32)],
        ),
        compiler_params=params(24),
        cost_estimate=cost(10_000_000_000, 25_000_000),
        name="expert_pass",
    )(b, w_in, c, gates)


def dbuf_kernel(t_ref, du_ref, w_ref, dg_ref, keep_ref, send_ref, acc):
    e = pl.program_id(0)
    last = pl.num_programs(0) - 1
    length = du_ref.shape[0]
    count = length // 4

    def chunk(n, carry):
        rows = pl.ds(pl.multiple_of(n * count, count), count)
        got = dot(du_ref[rows, :], w_ref[...], NT)
        total = jnp.where(e == 0, got, acc[rows, :] + got)
        acc[rows, :] = total

        @pl.when(e == last)
        def _():
            r = t_ref[0] ^ n
            tail = jnp.concatenate(
                [dg_ref[:, rows], jnp.zeros((8, total.shape[1] - count), f32)], axis=1
            )

            @pl.when(r % 2 == 0)
            def _():
                keep_ref[r // 2, 0:count, :] = total
                keep_ref[r // 2, count : count + 8, :] = tail

            @pl.when(r % 2 == 1)
            def _():
                send_ref[r // 2, 0:count, :] = total
                send_ref[r // 2, count : count + 8, :] = tail

        return carry

    lax.fori_loop(0, 4, chunk, 0)


def dbuf(t, du, w_in, dg):
    length = du.shape[0]
    experts, width, hidden = w_in.shape
    sds = jax.ShapeDtypeStruct((2, length // 4 + 8, width), f32)
    whole = pl.BlockSpec((2, length // 4 + 8, width), lambda i: (0, 0, 0))
    return pl.pallas_call(
        dbuf_kernel,
        out_shape=(sds, sds),
        grid_spec=pltpu.PrefetchScalarGridSpec(
            num_scalar_prefetch=0,
            grid=(experts,),
            in_specs=[
                SM,
                pl.BlockSpec((length, hidden), lambda i: (0, i)),
                pl.BlockSpec((None, width, hidden), lambda i: (i, 0, 0)),
                pl.BlockSpec((8, length), lambda i: (0, 0)),
            ],
            out_specs=[whole, whole],
            scratch_shapes=[pltpu.VMEM((length, width), f32)],
        ),
        compiler_params=params(28),
        cost_estimate=cost(4_800_000_000, 18_000_000),
        name="dbuf",
    )(t, du, w_in, dg)


def moe_kernel(t_ref, gg_ref, w_ref, h_ref, keep_ref, send_ref, acc):
    e = pl.program_id(0)
    last = pl.num_programs(0) - 1
    length = gg_ref.shape[0]
    cols = h_ref.shape[1] // 4
    step = 256

    def chunk(n, carry):
        rows = pl.ds(pl.multiple_of(n * step, step), step)
        got = dot(gg_ref[rows, :], w_ref[...])
        acc[rows, :] = jnp.where(e == 0, got, acc[rows, :] + got)
        return carry

    lax.fori_loop(0, length // step, chunk, 0)

    @pl.when(e == last)
    def _():
        t = t_ref[0]
        for k in range(4):
            r = t ^ k
            part = slice(k * cols, (k + 1) * cols)
            for side in range(2):
                rows = slice(side * (length // 2), (side + 1) * (length // 2))
                lanes = slice(side * cols, (side + 1) * cols)

                @pl.when(r == 0)
                def _():
                    keep_ref[0, :, lanes] = acc[rows, part] + h_ref[rows, part]

                @pl.when(r == 2)
                def _():
                    keep_ref[1, :, lanes] = acc[rows, part]

                @pl.when(r % 2 == 1)
                def _():
                    send_ref[r // 2, :, lanes] = acc[rows, part]


def moe(t, gg, w_out, h):
    length, width = h.shape
    experts, hidden, _ = w_out.shape
    shape = (2, length // 2, width // 2)
    sds = jax.ShapeDtypeStruct(shape, f32)
    whole = pl.BlockSpec(shape, lambda i: (0, 0, 0))
    return pl.pallas_call(
        moe_kernel,
        out_shape=(sds, sds),
        grid_spec=pltpu.PrefetchScalarGridSpec(
            num_scalar_prefetch=0,
            grid=(experts,),
            in_specs=[
                SM,
                pl.BlockSpec((length, hidden), lambda i: (0, i)),
                pl.BlockSpec((None, hidden, width), lambda i: (i, 0, 0)),
                pl.BlockSpec((length, width), lambda i: (0, 0)),
            ],
            out_specs=[whole, whole],
            scratch_shapes=[pltpu.VMEM((length, width), f32)],
        ),
        compiler_params=params(32),
        cost_estimate=cost(4_800_000_000, 18_000_000),
        name="moe",
    )(t, gg, w_out, h)


def norm2_kernel(
    t_ref, k0_ref, r0_ref, x0_ref, h_ref, b_ref, gates_ref, probs_ref, c_ref, gain_ref, rt_ref,
    dh_ref, small_ref,
):
    count, width = dh_ref.shape
    experts = probs_ref.shape[1]
    ext = k0_ref[...] + r0_ref[...] + x0_ref[...]
    db = ext[:count]
    dgt = ext[count : count + 8, :count]
    dg = jnp.concatenate([dgt, jnp.zeros((120, count), f32)], 0).T[:, :experts]
    probs = probs_ref[...]
    dprobs = jnp.where(gates_ref[...] > 0.0, dg, 0.0)
    dlogit = probs * (dprobs - jnp.sum(probs * dprobs, axis=1, keepdims=True))
    b = b_ref[...].astype(f32)
    rows = []
    for e in range(experts):
        col = dlogit[:, e : e + 1]
        db = db + col * rt_ref[e : e + 1, :].astype(f32)
        rows.append(jnp.sum(b * col, axis=0, keepdims=True))
    h = h_ref[...]
    r = lax.rsqrt(jnp.mean(h * h, axis=1, keepdims=True) + EPS)
    rows.append(jnp.sum(db * h * r, axis=0, keepdims=True))
    rows.append(jnp.zeros((8 - experts - 1, width), f32))
    small_ref[...] = jnp.concatenate(rows, axis=0)
    weighted = db * gain_ref[...]
    inner = jnp.mean(weighted * h, axis=1, keepdims=True)
    dh_ref[...] = c_ref[...].astype(f32) + r * weighted - h * (r * r * r) * inner


def norm2_back(t, keep, got, across, h, b, gates, probs, cotangent, gain, router):
    length, width = h.shape
    count = length // 4
    experts = router.shape[1]
    first = pl.BlockSpec((None, count + 8, width), lambda i, t: (0, 0, 0))
    sds = jax.ShapeDtypeStruct

    def mine(cols):
        return pl.BlockSpec((count, cols), lambda i, t: (t[0], 0))

    return pl.pallas_call(
        norm2_kernel,
        out_shape=(sds((count, width), f32), sds((8, width), f32)),
        grid_spec=pltpu.PrefetchScalarGridSpec(
            num_scalar_prefetch=1,
            grid=(1,),
            in_specs=[
                first,
                first,
                pl.BlockSpec((count + 8, width), lambda i, t: (0, 0)),
                mine(width),
                mine(width),
                mine(experts),
                mine(experts),
                mine(width),
                pl.BlockSpec((1, width), lambda i, t: (0, 0)),
                pl.BlockSpec((experts, width), lambda i, t: (0, 0)),
            ],
            out_specs=[
                pl.BlockSpec((count, width), lambda i, t: (0, 0)),
                pl.BlockSpec((8, width), lambda i, t: (0, 0)),
            ],
        ),
        compiler_params=params(24),
        cost_estimate=cost(10_000_000, 5_000_000),
        name="norm2_back",
    )(t, keep, got, across, h, b, gates, probs, cotangent, gain.reshape(1, width), router.T)


def da_kernel(t_ref, w_ref, g_ref, xt_ref, gain_ref, r1_ref, keep_ref, send_ref, dots_ref, dgain_ref):
    count = keep_ref.shape[1]
    length = keep_ref.shape[2]
    dots = jnp.zeros((1, length), f32)
    r1 = r1_ref[...]
    for k in range(4):
        rows = slice(k * count, (k + 1) * count)
        part = dot(w_ref[0, rows, :], g_ref[0])
        for c in range(1, 3):
            part = part + dot(w_ref[c, rows, :], g_ref[c])
        dx = part * xt_ref[rows, :].astype(f32)
        dots = dots + jnp.sum(dx * gain_ref[rows, :], axis=0, keepdims=True)
        dgain_ref[rows, :] = jnp.sum(dx * r1, axis=1, keepdims=True)
        r = t_ref[0] ^ k

        @pl.when(r % 2 == 0)
        def _():
            keep_ref[r // 2] = part

        @pl.when(r % 2 == 1)
        def _():
            send_ref[r // 2] = part

    dots_ref[...] = dots


def da_pass(t, w, g, xt, gain, r1):
    width, length = xt.shape
    sds = jax.ShapeDtypeStruct
    shape = sds((2, width // 4, length), f32)
    return pl.pallas_call(
        da_kernel,
        out_shape=(shape, shape, sds((1, length), f32), sds((width, 1), f32)),
        in_specs=[SM] + [VM] * 5,
        out_specs=[VM] * 4,
        compiler_params=params(32),
        cost_estimate=cost(900_000_000, 6_000_000),
        name="da_pass",
    )(t, w, g, xt, gain.reshape(width, 1), r1)


def last_kernel(
    t_ref, k0_ref, r0_ref, x0_ref, xt_ref, gain_ref, r1_ref, dots_ref, d0, d1, d2, d3, out_ref
):
    cols = out_ref.shape[1]
    count, width = d0.shape
    t = t_ref[0]
    r1 = r1_ref[...]
    da = k0_ref[...] + r0_ref[...] + x0_ref[...]
    rows = pl.ds(pl.multiple_of(t * cols, cols), cols)
    x = xt_ref[rows, :].astype(f32)
    norm = r1 * (da * gain_ref[rows, :]) - x * (r1 * r1 * r1) * (dots_ref[...] * (1.0 / width))
    turned = norm.T
    out_ref[...] = turned
    for k in range(4):

        @pl.when(t == k)
        def _():
            for r, d in enumerate((d0, d1, d2, d3)):
                at = (k ^ r) * count
                out_ref[at : at + count, :] += d[:, k * cols : (k + 1) * cols]


def last_pass(t, keep, got, across, xt, gain, r1, dots, shards):
    width, length = xt.shape
    sds = jax.ShapeDtypeStruct
    return pl.pallas_call(
        last_kernel,
        out_shape=sds((length, width // 4), f32),
        in_specs=[SM] + [VM] * 11,
        out_specs=VM,
        compiler_params=params(32),
        cost_estimate=cost(10_000_000, 6_000_000),
        name="last_pass",
    )(t, keep[0], got[0], across, xt, gain.reshape(width, 1), r1, dots, *shards)


def ring_order(n):
    return list(range(0, n, 2)) + list(range(n - 1, 0, -2))


def ring_sums(parts, n):
    order = ring_order(n)
    place = jnp.asarray([order.index(i) for i in range(n)], jnp.int32)[lax.axis_index("dp")]
    table = jnp.asarray(order, jnp.int32)

    def piece(array, direction, step):
        rows = array.shape[0] // n
        at = table[(place - direction * (1 + step)) % n]
        return lax.dynamic_slice_in_dim(array, at * rows, rows, 0)

    moves = {
        1: [(order[i], order[(i + 1) % n]) for i in range(n)],
        -1: [(order[i], order[(i - 1) % n]) for i in range(n)],
    }
    held = [piece(a, d, 0) for a, d in parts]
    for step in range(1, n):
        came = [lax.ppermute(x, "dp", moves[d]) for x, (_, d) in zip(held, parts)]
        held = [x + piece(a, d, step) for x, (a, d) in zip(came, parts)]
    return held


def sum_over_dp(parts, n):
    rows = parts[0][0].shape[0] // n
    if n % 2 == 0 and n <= 16 and rows % 8 == 0:
        return ring_sums(parts, n)
    return [lax.psum_scatter(a, "dp", scatter_dimension=0, tiled=True) for a, _ in parts]


def on_device(
    dp_count, tokens, cotangent, gain_attn, prefix_len, bucket_ids, pos_bias, w_qkv, w_attn_out,
    gain_ffn, w_router, expert_ids, w_expert_in, w_expert_out,
):
    length, width = tokens.shape
    heads = pos_bias.shape[1]
    flat = w_attn_out.shape[0]
    experts, _, hidden = w_expert_in.shape
    t = lax.axis_index("tensor").astype(jnp.int32).reshape(1)

    def core(x):
        return lax.ppermute(x, "tensor", CORE)

    def across(x):
        return lax.ppermute(x, "tensor", ACROSS)

    wo = w_attn_out.astype(f32)
    wo_x = across(wo)
    wos = (w_attn_out, core(wo), wo_x, core(wo_x))
    ids_rev = jnp.concatenate([bucket_ids[::-1], bucket_ids[:1]])[None, :]

    a, q, kt, v, os, o = attn_fwd(prefix_len, tokens, gain_attn, w_qkv, ids_rev, pos_bias)
    o_x = across(o)
    o_shards = (o, core(o), o_x, core(o_x))
    c_w = jnp.einsum("ld,efd->lef", cotangent, w_expert_out, preferred_element_type=f32)
    c_w = c_w.astype(bf16).reshape(length, experts * hidden)
    h, b, gates, probs = proj(tokens, o_shards, wos, gain_ffn, w_router, expert_ids)
    gg, du, dg = expert_pass(b, w_expert_in, c_w, gates)

    grad_out_t = dot(cotangent, gg, TN)
    grad_in = dot(b, du, TN)
    mid = (experts // 2) * hidden

    db_keep, db_send = dbuf(t, du, w_expert_in, dg)
    db_got = core(db_send)
    db_across = across(db_keep[1] + db_got[1])
    dh, small_ffn = norm2_back(
        t, db_keep, db_got, db_across, h, b, gates, probs, cotangent, gain_ffn, w_router
    )
    dh_x = across(dh)
    dh_shards = (dh, core(dh), dh_x, core(dh_x))

    y_keep, y_send = moe(t, gg, w_expert_out, h)
    y_got = core(y_send)
    y_across = across(y_keep[1] + y_got[1])
    packed = y_keep[0] + y_got[0] + y_across
    cols = width // 4
    output = jnp.concatenate([packed[:, :cols], packed[:, cols:]], axis=0).astype(bf16)

    g, dpb = attn_bwd(
        prefix_len, t, dh_shards, w_attn_out, q, kt, v, os, ids_rev, pos_bias
    )
    g = g.reshape(3, flat, length)
    xt = tokens.T
    xf = tokens.astype(f32)
    r1 = lax.rsqrt(jnp.mean(xf * xf, axis=1) + EPS)[None, :]
    da_keep, da_send, dots, dgain = da_pass(t, w_qkv, g, xt, gain_attn, r1)

    pad = jnp.zeros((8, length - width), f32)
    small = jnp.concatenate([small_ffn, pad], axis=1)
    small = jnp.concatenate(
        [small[: experts + 1], dots, jnp.pad(dgain.T, ((0, 0), (0, length - width))), small[-1:]], axis=0
    )
    small = small + core(small)
    small = small + across(small)
    dots = small[experts + 1 : experts + 2]

    da_got = core(da_send)
    da_across = across(da_keep[1] + da_got[1])
    d_tokens = last_pass(t, da_keep, da_got, da_across, xt, gain_attn, r1, dots, dh_shards)

    d_all = jnp.zeros((length, width), bf16)
    count = length // 4
    for r, d in enumerate(dh_shards):
        d_all = lax.dynamic_update_slice_in_dim(d_all, d.astype(bf16), (t[0] ^ r) * count, 0)
    o_flat = jnp.concatenate([o[:, :flat], o[:, flat:]], axis=0).astype(bf16)
    grad_wo_t = dot(d_all, o_flat, TN)
    grad_qkv = jnp.einsum("ld,cfl->dcf", a, g, preferred_element_type=f32).reshape(width, 3 * flat)
    rows = width // dp_count
    columns = [small[: experts + 1, :width].T, small[experts + 2 : experts + 3, :width].T]
    if rows % 8 == 0:
        bias_flat = dpb.reshape(-1)
        reps = -(-bias_flat.shape[0] // rows)
        bias_cols = jnp.pad(bias_flat, (0, reps * rows - bias_flat.shape[0])).reshape(reps, rows).T
        columns.append(jnp.tile(bias_cols, (dp_count, 1)))
    tail = jnp.concatenate(columns, axis=1)
    tail = jnp.pad(tail, ((0, 0), (0, 128 - tail.shape[1])))

    sums = sum_over_dp(
        [
            (grad_out_t[:, :mid], 1),
            (grad_out_t[:, mid:], -1),
            (grad_in[:, :mid], 1),
            (grad_in[:, mid:], -1),
            (jnp.concatenate([grad_qkv[:, : 2 * flat], tail], axis=1), 1),
            (jnp.concatenate([grad_qkv[:, 2 * flat :], grad_wo_t], axis=1), -1),
        ],
        dp_count,
    )
    g_out = jnp.concatenate(sums[0:2], axis=1).T.reshape(experts, hidden, rows)
    g_in = jnp.concatenate(sums[2:4], axis=1).reshape(rows, experts, hidden).transpose(1, 0, 2)
    g_qkv = jnp.concatenate([sums[4][:, : 2 * flat], sums[5][:, :flat]], axis=1)
    g_qkv = g_qkv.reshape(rows, 3, flat).transpose(1, 0, 2)
    g_wo = sums[5][:, flat:].T
    g_small = sums[4][:, 2 * flat :]
    if rows % 8 == 0:
        bias = g_small[:, experts + 2 : experts + 2 + reps].T.reshape(-1)[: dpb.size]
        g_bias = bias.reshape(dpb.shape)
    else:
        g_bias = lax.psum(dpb, "dp")
    return (
        output, d_tokens, g_small[:, experts + 1], g_bias, g_qkv, g_wo, g_small[:, experts],
        g_small[:, :experts], g_in, g_out,
    )


def solution(mesh):
    in_specs = (
        P("dp", None), P("dp", None), P(), P("dp"), P(), P(None, "tensor"), P(None, None, "tensor"),
        P("tensor", None), P(), P(), P("dp", None), P(None, None, "tensor"), P(None, "tensor", None),
    )
    out_specs = (
        P("dp", "tensor"), P("dp", "tensor"), P("dp"), P(None, "tensor"), P(None, "dp", "tensor"),
        P("tensor", "dp"), P("dp"), P("dp", None), P(None, "dp", "tensor"), P(None, "tensor", "dp"),
    )

    def body(*args):
        return on_device(mesh.shape["dp"], *args)

    return jax.shard_map(body, mesh=mesh, in_specs=in_specs, out_specs=out_specs, check_vma=False)
```
